128 devices in a mesh: wide: 32 (over x, z, core), narrow: 4 (over y).
Axes of the slice: x: 4, y: 4, z: 4, core: 2. Of those that a mesh axis runs over, the one named last changes fastest.
Arguments:
- pressure: bfloat16 [16384, 32768], P(None, ('wide', 'narrow')), may hold values from -6 to 6
- weights: float32 [32768], P(('wide', 'narrow')), may hold values from 7.6293945e-06 to 0.00012207031
- green_table: float32 [4, 2, 1024, 32768], P(None, None, None, ('wide', 'narrow')), may hold values from -0.03125 to 0.03125
- starts: int32 [127], replicated, may hold values from 0 to 16128, as said below
- bin_index: int32 [4], replicated, may hold values from 1 to 127, as said below
Outputs:
- mic_power: float32 [1024, 4], P(('wide', 'narrow'))
The draws below stay inside these ranges and needn't reach their ends.
Inputs may be any that keep to these rules, and one draw needn't show every extreme that they name: Block k starts within 32 samples of k * 128; the first block starts at 0 and the last at 16128. `bin_index`: distinct bins; the lowest is 1 and the highest 256 // 2 - 1.
All inputs are finite; a program needn't handle non-finite values.
Results may differ from the reference program's by a relative error of at most 0.0018.
Values sent between devices are 32-bit elements; how exact they have to be, the bound alone decides.
No kernel may reach another device: no remote copies, remote signals or barrier semaphores. Data moves between devices by JAX's collectives and lax.ppermute only.
A program may use at most 128 MiB of HBM per device.

```python
import math
import jax
import jax.numpy as jnp
from jax import lax

NFFT = 256
HOP = 128
NB = 127
BINS = 4
MODES = 4
ITERS = 8
MICS = 1024
SAMPLES = 16384
POINTS = 32768


def draw_starts(key, part):
    nominal = jnp.arange(NB, dtype=jnp.int32) * HOP
    jitter = jax.random.randint(key, (NB,), -(HOP // 4), HOP // 4 + 1, dtype=jnp.int32)
    placed = jnp.clip(nominal + jitter, 0, SAMPLES - NFFT)
    placed = placed.at[0].set(0)
    placed = placed.at[NB - 1].set(SAMPLES - NFFT)
    return placed.astype(jnp.int32)


def draw_bin_index(key, part):
    key_pick = jax.random.fold_in(key, 11)
    key_order = jax.random.fold_in(key, 23)
    middle = jax.random.permutation(key_pick, NFFT // 2 - 3) + 2
    ends = jnp.array([1, NFFT // 2 - 1], dtype=jnp.int32)
    chosen = jnp.concatenate([ends, middle[:BINS - 2].astype(jnp.int32)])
    order = jax.random.permutation(key_order, BINS)
    return chosen[order].astype(jnp.int32)


def levels(key, dims, cuts, least, largest):
    factor_of = 1.0
    for position, shards_of in cuts:
        heights = jax.random.uniform(jax.random.fold_in(jax.random.fold_in(key, 6), position), (shards_of,), jnp.float32, least / len(cuts), largest / len(cuts))
        factor_of = factor_of * jnp.repeat(jnp.exp(heights), dims[position] // shards_of).reshape((-1,) + (1,) * (len(dims) - 1 - position))
    return factor_of


def bell_draw(stream_key, extent, scale, limit, pieces=(), kind=jnp.bfloat16):
    drawn = jax.random.normal(stream_key, extent, jnp.float32) * scale
    if len(pieces) > 0:
        drawn = levels(stream_key, extent, pieces, -0.22, 0.18) * drawn
    return jnp.clip(drawn, min=-limit, max=limit).astype(kind)


def setup_inputs(seed: int = 0) -> dict:
    seeds = jax.random.split(jax.random.key(seed), 6)
    pressure = bell_draw(seeds[0], (SAMPLES, POINTS), 1.0, 6.0, ((1, 128),))
    weights = jnp.clip(jnp.exp(math.log(0.00012207031) - 2.7725887 * jax.random.uniform(seeds[1], (POINTS,), jnp.float32) ** levels(seeds[1], (POINTS,), ((0, 128),), -0.2, 0.2)), 7.62939453125e-06, 0.00012207031)
    green_table = bell_draw(seeds[2], (BINS, 2, MICS, POINTS), POINTS ** -0.5, 0.03125, ((3, 128),), jnp.float32)
    starts = draw_starts(jax.random.fold_in(seeds[5], 71), 0)
    bin_index = draw_bin_index(jax.random.fold_in(seeds[5], 71), 0)
    return dict(pressure=pressure, weights=weights, green_table=green_table, starts=starts, bin_index=bin_index)


def spectrum_table(bin_index):
    sample = jnp.arange(NFFT, dtype=jnp.int32)
    window = 0.5 - 0.5 * jnp.cos(2.0 * math.pi * sample.astype(jnp.float32) / NFFT)
    norm_scale = 1.0 / jnp.sqrt(jnp.sum(window * window))
    turns = bin_index[:, None] * sample[None, :] % NFFT
    phases = 2.0 * math.pi * turns.astype(jnp.float32) / NFFT
    cos_rows = norm_scale * window[None, :] * jnp.cos(phases)
    sin_rows = -norm_scale * window[None, :] * jnp.sin(phases)
    return jnp.concatenate([cos_rows, sin_rows], 0).astype(jnp.bfloat16)

def block_spectra(pressure, starts, dft_table):

    def one_block(first):
        block = lax.dynamic_slice_in_dim(pressure, first, NFFT, 0)
        return jnp.dot(dft_table, block, preferred_element_type=jnp.float32)
    spectra = lax.map(one_block, starts)
    return (spectra[:, :BINS], spectra[:, BINS:])

def gram_of(real_part, imag_part, weights):
    high = lax.Precision.HIGHEST
    wreal = real_part * weights
    wimag = imag_part * weights
    gram_re = jnp.einsum('bfp,cfp->fbc', wreal, real_part, precision=high) + jnp.einsum('bfp,cfp->fbc', wimag, imag_part, precision=high)
    gram_im = jnp.einsum('bfp,cfp->fbc', wreal, imag_part, precision=high) - jnp.einsum('bfp,cfp->fbc', wimag, real_part, precision=high)
    return jnp.stack([gram_re, gram_im], 0)

def orthonormal(image_re, image_im):
    done_re = []
    done_im = []
    for column in range(image_re.shape[-1]):
        vec_re = image_re[..., column]
        vec_im = image_im[..., column]
        for earlier in range(column):
            prev_re = done_re[earlier]
            prev_im = done_im[earlier]
            coef_re = lax.optimization_barrier(jnp.sum(prev_re * vec_re + prev_im * vec_im, axis=-1, keepdims=True))
            coef_im = lax.optimization_barrier(jnp.sum(prev_re * vec_im - prev_im * vec_re, axis=-1, keepdims=True))
            vec_re = vec_re - (coef_re * prev_re - coef_im * prev_im)
            vec_im = vec_im - (coef_re * prev_im + coef_im * prev_re)
        inverse = lax.rsqrt(lax.optimization_barrier(jnp.sum(vec_re * vec_re + vec_im * vec_im, axis=-1, keepdims=True)) + 1e-06)
        done_re.append(vec_re * inverse)
        done_im.append(vec_im * inverse)
    return (jnp.stack(done_re, -1), jnp.stack(done_im, -1))

def leading_modes(gram):
    high = lax.Precision.HIGHEST
    gram_re = gram[0]
    gram_im = gram[1]
    blocks = gram_re.shape[-1]
    rowpos = jnp.arange(blocks, dtype=jnp.float32) + 0.5
    colpos = jnp.arange(MODES, dtype=jnp.float32) + 1.0
    start_basis = jnp.cos(math.pi * rowpos[:, None] * colpos[None, :] / blocks)
    basis_re = jnp.broadcast_to(start_basis, (gram_re.shape[0], blocks, MODES))
    basis_im = jnp.zeros_like(basis_re)
    for sweep in range(ITERS):
        image_re = jnp.einsum('fbc,fck->fbk', gram_re, basis_re, precision=high) - jnp.einsum('fbc,fck->fbk', gram_im, basis_im, precision=high)
        image_im = jnp.einsum('fbc,fck->fbk', gram_re, basis_im, precision=high) + jnp.einsum('fbc,fck->fbk', gram_im, basis_re, precision=high)
        basis_re, basis_im = orthonormal(image_re, image_im)
    return (basis_re, basis_im)

def reference(pressure, weights, green_table, starts, bin_index):
    high = lax.Precision.HIGHEST
    dft_table = spectrum_table(bin_index)
    real_part, imag_part = block_spectra(pressure, starts, dft_table)
    basis_re, basis_im = leading_modes(gram_of(real_part, imag_part, weights))
    shape_re = jnp.einsum('bfp,fbk->fpk', real_part, basis_re, precision=high) - jnp.einsum('bfp,fbk->fpk', imag_part, basis_im, precision=high)
    shape_im = jnp.einsum('bfp,fbk->fpk', real_part, basis_im, precision=high) + jnp.einsum('bfp,fbk->fpk', imag_part, basis_re, precision=high)
    green_re = green_table[:, 0]
    green_im = green_table[:, 1]
    amp_re = jnp.einsum('fmp,fpk->mfk', green_re, shape_re, precision=high) - jnp.einsum('fmp,fpk->mfk', green_im, shape_im, precision=high)
    amp_im = jnp.einsum('fmp,fpk->mfk', green_re, shape_im, precision=high) + jnp.einsum('fmp,fpk->mfk', green_im, shape_re, precision=high)
    return lax.optimization_barrier(jnp.sum(amp_re * amp_re + amp_im * amp_im, axis=-1))
```

```python
import math

import jax
import jax.numpy as jnp
import numpy as np
from jax import lax
from jax.experimental import pallas as pl
from jax.experimental.pallas import tpu as pltpu
from jax.sharding import PartitionSpec as P

NFFT = 256
NB = 127
BINS = 4
MODES = 4
ITERS = 8
MICS = 1024
SAMPLES = 16384
DEVICES = 128
LOCAL = 256
STEP_CHUNKS = 8
STEPS = SAMPLES // (NFFT * STEP_CHUNKS)
AXES = ("wide", "narrow")
NT = (((1,), (1,)), ((), ()))
NN = (((1,), (0,)), ((), ()))
BF = jnp.bfloat16
F32 = jnp.float32


def split(x):
    hi = x.astype(BF)
    return hi, (x - hi.astype(F32)).astype(BF)


def dot(a, b, dims):
    return lax.dot_general(a, b, dims, preferred_element_type=F32)


def gram_kernel(starts_ref, bins_ref, pressure_ref, weights_ref, gram_ref, high_ref, low_ref, table_ref, q_ref):
    step = pl.program_id(0)

    @pl.when(step == 0)
    def _():
        row = lax.broadcasted_iota(jnp.int32, (8, NFFT), 0)
        time = lax.broadcasted_iota(jnp.int32, (8, NFFT), 1)
        which = row & 3
        bins = jnp.where(
            which == 0,
            bins_ref[0],
            jnp.where(which == 1, bins_ref[1], jnp.where(which == 2, bins_ref[2], bins_ref[3])),
        )
        window = 0.5 - 0.5 * jnp.cos(2.0 * math.pi * time.astype(F32) / NFFT)
        scaled = np.float32(1.0 / math.sqrt(0.375 * NFFT)) * window
        phase = 2.0 * math.pi * ((bins * time) & (NFFT - 1)).astype(F32) / NFFT
        rows = jnp.where(row < 4, scaled * jnp.cos(phase), -scaled * jnp.sin(phase))
        table_ref[...] = rows.astype(BF).astype(F32)
        q_ref[...] = jnp.zeros_like(q_ref)

    table = table_ref[...]
    time = lax.broadcasted_iota(jnp.int32, (8, NFFT), 1)
    first = 2 * STEP_CHUNKS * step - 2
    rolled = []
    begins = []
    for k in range(2 * STEP_CHUNKS + 3):
        block = first + k
        start = starts_ref[jnp.clip(block, 0, NB - 1)]
        rolled.append(pltpu.roll(table, start & (NFFT - 1), 1))
        begins.append(jnp.where((block >= 0) & (block < NB), start, 1 << 20))
    for c in range(STEP_CHUNKS):
        base = (step * STEP_CHUNKS + c) * NFFT
        parts = []
        for k in range(5):
            at = time + (base - begins[2 * c + k])
            parts.append(jnp.where((at >= 0) & (at < NFFT), rolled[2 * c + k], 0.0))
        parts.append(jnp.zeros((8, NFFT), F32))
        lhs = jnp.concatenate(parts, 0).astype(BF)
        got = dot(lhs, pressure_ref[c * NFFT : (c + 1) * NFFT, :], NN)
        rows = pl.ds(pl.multiple_of(step * (16 * STEP_CHUNKS) + 16 * c, 8), 40)
        q_ref[0, rows, :] += got[:40, :128]
        q_ref[1, rows, :] += got[:40, 128:]

    @pl.when(step == STEPS - 1)
    def _():
        weights = weights_ref[...]
        upper = lax.broadcasted_iota(jnp.int32, (128, 128), 1) >= lax.broadcasted_iota(jnp.int32, (128, 128), 0)
        for f in range(BINS):
            halves = [
                jnp.concatenate([q_ref[h, pl.ds(16 + g, 128, stride=8), :] for g in (f, 4 + f)], 0)
                for h in range(2)
            ]
            both = jnp.concatenate(halves, 1)
            hi, lo = split(both)
            high_ref[f] = hi
            low_ref[f] = lo
            whi, wlo = split(both * weights)
            prod = dot(whi, hi, NT) + dot(wlo, hi, NT) + dot(whi, lo, NT)
            gram_re = prod[:128, :128] + prod[128:, 128:]
            gram_im = prod[:128, 128:] - prod[128:, :128]
            gram_ref[f * 128 : (f + 1) * 128, :] = jnp.where(upper, gram_re, gram_im)


def local_gram(pressure, weights, starts, bin_index):
    return pl.pallas_call(
        gram_kernel,
        out_shape=(
            jax.ShapeDtypeStruct((BINS * 128, 128), F32),
            jax.ShapeDtypeStruct((BINS, 256, LOCAL), BF),
            jax.ShapeDtypeStruct((BINS, 256, LOCAL), BF),
        ),
        grid_spec=pltpu.PrefetchScalarGridSpec(
            num_scalar_prefetch=2,
            grid=(STEPS,),
            in_specs=[
                pl.BlockSpec((NFFT * STEP_CHUNKS, LOCAL), lambda i, s, b: (i, 0)),
                pl.BlockSpec((1, LOCAL), lambda i, s, b: (0, 0)),
            ],
            out_specs=[
                pl.BlockSpec((BINS * 128, 128), lambda i, s, b: (0, 0)),
                pl.BlockSpec((BINS, 256, LOCAL), lambda i, s, b: (0, 0, 0)),
                pl.BlockSpec((BINS, 256, LOCAL), lambda i, s, b: (0, 0, 0)),
            ],
            scratch_shapes=[pltpu.VMEM((8, NFFT), F32), pltpu.VMEM((2, 1048, 128), F32)],
        ),
        compiler_params=pltpu.CompilerParams(vmem_limit_bytes=24 << 20),
        cost_estimate=pl.CostEstimate(flops=800_000_000, transcendentals=0, bytes_accessed=10_000_000),
        name="gram",
    )(starts, bin_index, pressure, weights.reshape(1, LOCAL))


def project_kernel(left_ref, right_ref, high_ref, low_ref, phigh_ref, plow_ref):
    hi = high_ref[0]
    lo = low_ref[0]
    for tile in range(4):
        cols = slice(tile * 256, (tile + 1) * 256)
        parts = []
        for side in range(2):
            halves = [
                jnp.concatenate([ref[0, side, pl.ds(2 * tile + i, 128, stride=8), :] for i in range(2)], 0)
                for ref in (left_ref, right_ref)
            ]
            mics = jnp.concatenate(halves, 1)
            ghi, glo = split(mics)
            parts.append(dot(hi, ghi, NT) + dot(lo, ghi, NT) + dot(hi, glo, NT))
        by_re, by_im = parts
        phi, plo = split(by_re[:128] - by_im[128:])
        phigh_ref[0, :128, cols] = phi
        plow_ref[0, :128, cols] = plo
        phi, plo = split(by_re[128:] + by_im[:128])
        phigh_ref[0, 128:, cols] = phi
        plow_ref[0, 128:, cols] = plo


def project(green_table, high, low):
    return pl.pallas_call(
        project_kernel,
        out_shape=(
            jax.ShapeDtypeStruct((BINS, 256, MICS), BF),
            jax.ShapeDtypeStruct((BINS, 256, MICS), BF),
        ),
        grid=(BINS,),
        in_specs=[
            pl.BlockSpec((1, 2, MICS, 128), lambda f: (f, 0, 0, 0)),
            pl.BlockSpec((1, 2, MICS, 128), lambda f: (f, 0, 0, 1)),
            pl.BlockSpec((1, 256, LOCAL), lambda f: (f, 0, 0)),
            pl.BlockSpec((1, 256, LOCAL), lambda f: (f, 0, 0)),
        ],
        out_specs=[
            pl.BlockSpec((1, 256, MICS), lambda f: (f, 0, 0)),
            pl.BlockSpec((1, 256, MICS), lambda f: (f, 0, 0)),
        ],
        compiler_params=pltpu.CompilerParams(vmem_limit_bytes=24 << 20),
        cost_estimate=pl.CostEstimate(flops=3_300_000_000, transcendentals=0, bytes_accessed=14_000_000),
        name="project",
    )(green_table, green_table, high, low)


def share_kernel(parts_ref, out_ref):
    total = parts_ref[0:8, :]
    for s in range(1, 64):
        total = total + parts_ref[8 * s : 8 * s + 8, :]
    total = total + pltpu.roll(total, 4, 0)
    for s in range(64):
        out_ref[8 * s : 8 * s + 8, :] = total


def share_sum(parts):
    return pl.pallas_call(
        share_kernel,
        out_shape=jax.ShapeDtypeStruct((512, 128), F32),
        compiler_params=pltpu.CompilerParams(vmem_limit_bytes=4 << 20),
        name="share",
    )(parts)


def modes_kernel(gram_ref, start_ref, phigh_hbm, plow_hbm, out_ref, phigh_ref, plow_ref, sems):
    fetch = [
        pltpu.make_async_copy(phigh_hbm, phigh_ref, sems.at[0]),
        pltpu.make_async_copy(plow_hbm, plow_ref, sems.at[1]),
    ]
    for copy in fetch:
        copy.start()
    col = lax.broadcasted_iota(jnp.int32, (128, 128), 1)
    row = lax.broadcasted_iota(jnp.int32, (128, 128), 0)
    lane_row = lax.broadcasted_iota(jnp.int32, (8, 128), 0)
    sign = jnp.where(lane_row < 4, 1.0, -1.0)
    mats = []
    for f in range(BINS):
        packed = gram_ref[f * 128 : (f + 1) * 128, :]
        flipped = packed.T
        gram_re = jnp.where(col >= row, packed, flipped)
        gram_im = jnp.where(col < row, packed, jnp.where(col > row, -flipped, 0.0))
        mats.append(split(jnp.concatenate([gram_re, gram_im], 1)))
    vecs = [start_ref[...]] * BINS
    for _ in range(ITERS):
        images = []
        for f in range(BINS):
            hi, lo = split(vecs[f])
            ghi, glo = mats[f]
            stacked = jnp.concatenate([hi, lo], 0)
            prod = dot(stacked, ghi, NN)
            prod = prod[:8] + prod[8:] + dot(hi, glo, NN)
            swapped = pltpu.roll(prod[:, 128:], 4, 0)
            images.append(prod[:, :128] + sign * swapped)
        for j in range(MODES):
            for f in range(BINS):
                y = images[f]
                vre = y[j : j + 1, :]
                vim = y[4 + j : 5 + j, :]
                turned = sign * pltpu.roll(y, 4, 0)
                coef = jnp.sum(y * vre + turned * vim, axis=1, keepdims=True)
                inverse = lax.rsqrt(coef[j : j + 1, :] + 1e-06)
                coef = jnp.broadcast_to(coef, (8, 128))
                scaled = coef * (inverse * inverse)
                cross = -sign * pltpu.roll(scaled, 4, 0)
                later = (lane_row & 3) > j
                here = (lane_row & 3) == j
                left = y - (scaled * vre + cross * vim)
                images[f] = jnp.where(later, left, jnp.where(here, y * inverse, y))
        vecs = images
    for copy in fetch:
        copy.wait()
    amps = []
    for f in range(BINS):
        y = vecs[f]
        turned = -sign * pltpu.roll(y, 4, 0)
        hi, lo = split(jnp.concatenate([y, turned], 1))
        prod = dot(jnp.concatenate([hi, lo], 0), phigh_ref[f], NN)
        amps.append(prod[:8] + prod[8:] + dot(hi, plow_ref[f], NN))
    for half in range(2):
        rows = []
        for i in range(4 * half, 4 * half + 4):
            for f in range(BINS):
                rows.append(amps[f][:, i * 128 : (i + 1) * 128])
        out_ref[:, half * 128 : (half + 1) * 128] = jnp.concatenate(rows, 0).T


def start_basis():
    rowpos = np.arange(NB) + 0.5
    colpos = np.arange(MODES) + 1.0
    basis = np.zeros((8, 128), np.float32)
    basis[:MODES, :NB] = np.cos(math.pi * colpos[:, None] * rowpos[None, :] / NB)
    return jnp.asarray(basis)


def amplitudes(gram, phigh, plow):
    return pl.pallas_call(
        modes_kernel,
        out_shape=jax.ShapeDtypeStruct((DEVICES, 256), F32),
        in_specs=[
            pl.BlockSpec((BINS * 128, 128), lambda: (0, 0)),
            pl.BlockSpec((8, 128), lambda: (0, 0)),
            pl.BlockSpec(memory_space=pl.ANY),
            pl.BlockSpec(memory_space=pl.ANY),
        ],
        scratch_shapes=[
            pltpu.VMEM((BINS, 256, MICS), BF),
            pltpu.VMEM((BINS, 256, MICS), BF),
            pltpu.SemaphoreType.DMA((2,)),
        ],
        compiler_params=pltpu.CompilerParams(vmem_limit_bytes=24 << 20),
        name="modes",
    )(gram, start_basis(), phigh, plow)


def power_kernel(parts_ref, out_ref):
    total = jnp.sum(parts_ref[...], axis=0, keepdims=True)
    square = jnp.broadcast_to(total * total, (8, 256))
    lane = lax.broadcasted_iota(jnp.int32, (8, 256), 1)
    mine = (lane >> 5) == lax.broadcasted_iota(jnp.int32, (8, 256), 0)
    cols = []
    for f in range(BINS):
        cols.append(jnp.sum(jnp.where(mine & (((lane >> 3) & 3) == f), square, 0.0), axis=1, keepdims=True))
    out_ref[...] = jnp.concatenate(cols, 1)


def power(parts):
    return pl.pallas_call(
        power_kernel,
        out_shape=jax.ShapeDtypeStruct((MICS // DEVICES, BINS), F32),
        compiler_params=pltpu.CompilerParams(vmem_limit_bytes=4 << 20),
        name="power",
    )(parts)


def exchange(x):
    return lax.all_to_all(x, AXES, 0, 0, tiled=True)


def on_device(pressure, weights, green_table, starts, bin_index):
    gram, high, low = local_gram(pressure, weights, starts, bin_index)
    parts = exchange(gram.reshape(DEVICES, 4, 128))
    phigh, plow = project(green_table, high, low)
    shared = share_sum(parts.reshape(512, 128))
    summed = exchange(shared.reshape(DEVICES, 4, 128)).reshape(512, 128)
    partial = amplitudes(summed, phigh, plow)
    return power(exchange(partial))


def solution(mesh):
    return jax.shard_map(
        on_device,
        mesh=mesh,
        in_specs=(
            P(None, AXES),
            P(AXES),
            P(None, None, None, AXES),
            P(),
            P(),
        ),
        out_specs=P(AXES, None),
        check_vma=False,
    )
```

```python
import math

import jax
import jax.numpy as jnp
import numpy as np
from jax import lax
from jax.experimental import pallas as pl
from jax.experimental.pallas import tpu as pltpu
from jax.sharding import PartitionSpec as P

NFFT = 256
NB = 127
BINS = 4
MODES = 4
ITERS = 8
MICS = 1024
SAMPLES = 16384
DEVICES = 128
LOCAL = 256
STEP_CHUNKS = 8
STEP_ROWS = NFFT * STEP_CHUNKS
STEPS = SAMPLES // STEP_ROWS
AXES = ("wide", "narrow")
NT = (((1,), (1,)), ((), ()))
NN = (((1,), (0,)), ((), ()))
BF = jnp.bfloat16
F32 = jnp.float32


def split(x):
    hi = x.astype(BF)
    return hi, (x - hi.astype(F32)).astype(BF)


def dot(a, b, dims):
    return lax.dot_general(a, b, dims, preferred_element_type=F32)


def gram_kernel(
    starts_hbm, bins_hbm, weights_hbm, pressure_hbm, gram_ref, high_ref, low_ref,
    starts_ref, bins_ref, weights_ref, pressure_ref, q_ref, small_sems, sems,
):
    small = [
        pltpu.make_async_copy(starts_hbm, starts_ref, small_sems.at[0]),
        pltpu.make_async_copy(bins_hbm, bins_ref, small_sems.at[1]),
        pltpu.make_async_copy(weights_hbm, weights_ref, small_sems.at[2]),
    ]

    def chunk_copy(step):
        rows = pl.ds(pl.multiple_of(step * STEP_ROWS, STEP_ROWS), STEP_ROWS)
        return pltpu.make_async_copy(pressure_hbm.at[rows, :], pressure_ref.at[rows, :], sems.at[step])

    for copy in small:
        copy.start()
    for step in range(STEPS):
        chunk_copy(step).start()

    q_ref[...] = jnp.zeros_like(q_ref)
    row = lax.broadcasted_iota(jnp.int32, (8, NFFT), 0)
    time = lax.broadcasted_iota(jnp.int32, (8, NFFT), 1)
    which = row & 3
    window = 0.5 - 0.5 * jnp.cos(2.0 * math.pi * time.astype(F32) / NFFT)
    scaled = np.float32(1.0 / math.sqrt(0.375 * NFFT)) * window
    for copy in small:
        copy.wait()
    bins = jnp.where(
        which == 0,
        bins_ref[0],
        jnp.where(which == 1, bins_ref[1], jnp.where(which == 2, bins_ref[2], bins_ref[3])),
    )
    phase = 2.0 * math.pi * ((bins * time) & (NFFT - 1)).astype(F32) / NFFT
    table = jnp.where(row < 4, scaled * jnp.cos(phase), -scaled * jnp.sin(phase))
    table = table.astype(BF).astype(F32)

    def one_step(step, carry):
        first = 2 * STEP_CHUNKS * step - 2
        rolled = []
        begins = []
        for k in range(2 * STEP_CHUNKS + 3):
            block = first + k
            start = starts_ref[jnp.clip(block, 0, NB - 1)]
            rolled.append(pltpu.roll(table, start & (NFFT - 1), 1))
            begins.append(jnp.where((block >= 0) & (block < NB), start, 1 << 20))
        chunk_copy(step).wait()
        for c in range(STEP_CHUNKS):
            base = (step * STEP_CHUNKS + c) * NFFT
            parts = []
            for k in range(5):
                at = time + (base - begins[2 * c + k])
                parts.append(jnp.where((at >= 0) & (at < NFFT), rolled[2 * c + k], 0.0))
            parts.append(jnp.zeros((8, NFFT), F32))
            lhs = jnp.concatenate(parts, 0).astype(BF)
            rows = pl.ds(pl.multiple_of(base, NFFT), NFFT)
            got = dot(lhs, pressure_ref[rows, :], NN)
            rows = pl.ds(pl.multiple_of(step * (16 * STEP_CHUNKS) + 16 * c, 8), 40)
            q_ref[0, rows, :] += got[:40, :128]
            q_ref[1, rows, :] += got[:40, 128:]
        return carry

    lax.fori_loop(0, STEPS, one_step, 0)

    weights = weights_ref[...]
    upper = lax.broadcasted_iota(jnp.int32, (128, 128), 1) >= lax.broadcasted_iota(jnp.int32, (128, 128), 0)
    for f in range(BINS):
        halves = [
            jnp.concatenate([q_ref[h, pl.ds(16 + g, 128, stride=8), :] for g in (f, 4 + f)], 0) for h in range(2)
        ]
        both = jnp.concatenate(halves, 1)
        hi, lo = split(both)
        high_ref[f] = hi
        low_ref[f] = lo
        whi, wlo = split(both * weights)
        prod = dot(whi, hi, NT) + dot(wlo, hi, NT) + dot(whi, lo, NT)
        gram_re = prod[:128, :128] + prod[128:, 128:]
        gram_im = prod[:128, 128:] - prod[128:, :128]
        gram_ref[f * 128 : (f + 1) * 128, :] = jnp.where(upper, gram_re, gram_im)


def in_hbm(x):
    return pltpu.with_memory_space_constraint(x, pltpu.HBM)


def local_gram(pressure, weights, starts, bin_index):
    hbm = pl.BlockSpec(memory_space=pltpu.HBM)
    return pl.pallas_call(
        gram_kernel,
        out_shape=(
            jax.ShapeDtypeStruct((BINS * 128, 128), F32),
            jax.ShapeDtypeStruct((BINS, 256, LOCAL), BF),
            jax.ShapeDtypeStruct((BINS, 256, LOCAL), BF),
        ),
        in_specs=[hbm] * 4,
        scratch_shapes=[
            pltpu.SMEM((NB,), jnp.int32),
            pltpu.SMEM((BINS,), jnp.int32),
            pltpu.VMEM((1, LOCAL), F32),
            pltpu.VMEM((SAMPLES, LOCAL), BF),
            pltpu.VMEM((2, 1048, 128), F32),
            pltpu.SemaphoreType.DMA((3,)),
            pltpu.SemaphoreType.DMA((STEPS,)),
        ],
        compiler_params=pltpu.CompilerParams(vmem_limit_bytes=24 << 20),
        cost_estimate=pl.CostEstimate(flops=800_000_000, transcendentals=0, bytes_accessed=10_000_000),
        name="gram",
    )(in_hbm(starts), in_hbm(bin_index), in_hbm(weights.reshape(1, LOCAL)), in_hbm(pressure))


def project_kernel(left_ref, right_ref, high_ref, low_ref, phigh_ref, plow_ref):
    hi = high_ref[0]
    lo = low_ref[0]
    for tile in range(4):
        cols = slice(tile * 256, (tile + 1) * 256)
        parts = []
        for side in range(2):
            halves = [
                jnp.concatenate([ref[0, side, pl.ds(2 * tile + i, 128, stride=8), :] for i in range(2)], 0)
                for ref in (left_ref, right_ref)
            ]
            mics = jnp.concatenate(halves, 1)
            ghi, glo = split(mics)
            parts.append(dot(hi, ghi, NT) + dot(lo, ghi, NT) + dot(hi, glo, NT))
        by_re, by_im = parts
        phi, plo = split(by_re[:128] - by_im[128:])
        phigh_ref[0, :128, cols] = phi
        plow_ref[0, :128, cols] = plo
        phi, plo = split(by_re[128:] + by_im[:128])
        phigh_ref[0, 128:, cols] = phi
        plow_ref[0, 128:, cols] = plo


def project(green_table, high, low):
    return pl.pallas_call(
        project_kernel,
        out_shape=(
            pltpu.HBM((BINS, 256, MICS), BF),
            pltpu.HBM((BINS, 256, MICS), BF),
        ),
        grid=(BINS,),
        in_specs=[
            pl.BlockSpec((1, 2, MICS, 128), lambda f: (f, 0, 0, 0)),
            pl.BlockSpec((1, 2, MICS, 128), lambda f: (f, 0, 0, 1)),
            pl.BlockSpec((1, 256, LOCAL), lambda f: (f, 0, 0)),
            pl.BlockSpec((1, 256, LOCAL), lambda f: (f, 0, 0)),
        ],
        out_specs=[
            pl.BlockSpec((1, 256, MICS), lambda f: (f, 0, 0)),
            pl.BlockSpec((1, 256, MICS), lambda f: (f, 0, 0)),
        ],
        compiler_params=pltpu.CompilerParams(vmem_limit_bytes=24 << 20),
        cost_estimate=pl.CostEstimate(flops=3_300_000_000, transcendentals=0, bytes_accessed=14_000_000),
        name="project",
    )(in_hbm(green_table), in_hbm(green_table), high, low)


def share_kernel(parts_ref, out_ref):
    total = parts_ref[0:8, :]
    for s in range(1, 64):
        total = total + parts_ref[8 * s : 8 * s + 8, :]
    total = total + pltpu.roll(total, 4, 0)
    for s in range(64):
        out_ref[8 * s : 8 * s + 8, :] = total


def share_sum(parts):
    return pl.pallas_call(
        share_kernel,
        out_shape=jax.ShapeDtypeStruct((512, 128), F32),
        compiler_params=pltpu.CompilerParams(vmem_limit_bytes=4 << 20),
        name="share",
    )(parts)


def modes_kernel(gram_ref, start_ref, phigh_hbm, plow_hbm, out_ref, phigh_ref, plow_ref, sems):
    fetch = [
        pltpu.make_async_copy(phigh_hbm, phigh_ref, sems.at[0]),
        pltpu.make_async_copy(plow_hbm, plow_ref, sems.at[1]),
    ]
    for copy in fetch:
        copy.start()
    col = lax.broadcasted_iota(jnp.int32, (128, 128), 1)
    row = lax.broadcasted_iota(jnp.int32, (128, 128), 0)
    lane_row = lax.broadcasted_iota(jnp.int32, (8, 128), 0)
    sign = jnp.where(lane_row < 4, 1.0, -1.0)
    mats = []
    for f in range(BINS):
        packed = gram_ref[f * 128 : (f + 1) * 128, :]
        flipped = packed.T
        gram_re = jnp.where(col >= row, packed, flipped)
        gram_im = jnp.where(col < row, packed, jnp.where(col > row, -flipped, 0.0))
        mats.append(split(jnp.concatenate([gram_re, gram_im], 1)))
    vecs = [start_ref[...]] * BINS
    for _ in range(ITERS):
        images = []
        for f in range(BINS):
            hi, lo = split(vecs[f])
            ghi, glo = mats[f]
            stacked = jnp.concatenate([hi, lo], 0)
            prod = dot(stacked, ghi, NN)
            prod = prod[:8] + prod[8:] + dot(hi, glo, NN)
            swapped = pltpu.roll(prod[:, 128:], 4, 0)
            images.append(prod[:, :128] + sign * swapped)
        for j in range(MODES):
            for f in range(BINS):
                y = images[f]
                vre = y[j : j + 1, :]
                vim = y[4 + j : 5 + j, :]
                turned = sign * pltpu.roll(y, 4, 0)
                coef = jnp.sum(y * vre + turned * vim, axis=1, keepdims=True)
                inverse = lax.rsqrt(coef[j : j + 1, :] + 1e-06)
                coef = jnp.broadcast_to(coef, (8, 128))
                scaled = coef * (inverse * inverse)
                cross = -sign * pltpu.roll(scaled, 4, 0)
                later = (lane_row & 3) > j
                here = (lane_row & 3) == j
                left = y - (scaled * vre + cross * vim)
                images[f] = jnp.where(later, left, jnp.where(here, y * inverse, y))
        vecs = images
    for copy in fetch:
        copy.wait()
    amps = []
    for f in range(BINS):
        y = vecs[f]
        turned = -sign * pltpu.roll(y, 4, 0)
        hi, lo = split(jnp.concatenate([y, turned], 1))
        prod = dot(jnp.concatenate([hi, lo], 0), phigh_ref[f], NN)
        amps.append(prod[:8] + prod[8:] + dot(hi, plow_ref[f], NN))
    for half in range(2):
        rows = []
        for i in range(4 * half, 4 * half + 4):
            for f in range(BINS):
                rows.append(amps[f][:, i * 128 : (i + 1) * 128])
        out_ref[pl.ds(half, 128, stride=2), :] = jnp.concatenate(rows, 0).T


def start_basis():
    rowpos = np.arange(NB) + 0.5
    colpos = np.arange(MODES) + 1.0
    basis = np.zeros((8, 128), np.float32)
    basis[:MODES, :NB] = np.cos(math.pi * colpos[:, None] * rowpos[None, :] / NB)
    return jnp.asarray(basis)


def amplitudes(gram, phigh, plow):
    return pl.pallas_call(
        modes_kernel,
        out_shape=jax.ShapeDtypeStruct((2 * DEVICES, 128), F32),
        in_specs=[pl.BlockSpec(memory_space=pltpu.VMEM)] * 2 + [pl.BlockSpec(memory_space=pltpu.HBM)] * 2,
        scratch_shapes=[
            pltpu.VMEM((BINS, 256, MICS), BF),
            pltpu.VMEM((BINS, 256, MICS), BF),
            pltpu.SemaphoreType.DMA((2,)),
        ],
        compiler_params=pltpu.CompilerParams(vmem_limit_bytes=24 << 20),
        name="modes",
    )(gram, start_basis(), in_hbm(phigh), in_hbm(plow))


def power_kernel(parts_ref, out_ref):
    total = parts_ref[0:8, :]
    for s in range(1, 32):
        total = total + parts_ref[8 * s : 8 * s + 8, :]
    total = total + pltpu.roll(total, 4, 0)
    total = total + pltpu.roll(total, 6, 0)
    square = total * total
    lane = lax.broadcasted_iota(jnp.int32, (8, 128), 1)
    row = lax.broadcasted_iota(jnp.int32, (8, 128), 0)
    mic = lax.broadcasted_iota(jnp.int32, (8, 8), 1)
    out = jnp.zeros((8, 8), F32)
    for half in range(2):
        source = jnp.broadcast_to(square[half : half + 1, :], (8, 128))
        for i in range(4):
            sums = jnp.sum(jnp.where((lane >> 3) == 4 * i + row, source, 0.0), axis=1, keepdims=True)
            out = jnp.where(mic == 4 * half + i, sums, out)
    out_ref[...] = out[:BINS, :]


def power(parts):
    return pl.pallas_call(
        power_kernel,
        out_shape=jax.ShapeDtypeStruct((BINS, MICS // DEVICES), F32),
        compiler_params=pltpu.CompilerParams(vmem_limit_bytes=4 << 20),
        name="power",
    )(parts).T


def exchange(x):
    return lax.all_to_all(x, AXES, 0, 0, tiled=True)


def on_device(pressure, weights, green_table, starts, bin_index):
    gram, high, low = local_gram(pressure, weights, starts, bin_index)
    parts = exchange(gram.reshape(DEVICES, 4, 128))
    phigh, plow = project(green_table, high, low)
    shared = share_sum(parts.reshape(512, 128))
    summed = exchange(shared.reshape(DEVICES, 4, 128)).reshape(512, 128)
    partial = amplitudes(summed, phigh, plow)
    return power(exchange(partial.reshape(DEVICES, 2, 128)).reshape(2 * DEVICES, 128))


def solution(mesh):
    return jax.shard_map(
        on_device,
        mesh=mesh,
        in_specs=(
            P(None, AXES),
            P(AXES),
            P(None, None, None, AXES),
            P(),
            P(),
        ),
        out_specs=P(AXES, None),
        check_vma=False,
    )
```

```python
import math

import jax
import jax.numpy as jnp
import numpy as np
from jax import lax
from jax.experimental import pallas as pl
from jax.experimental.pallas import tpu as pltpu
from jax.sharding import PartitionSpec as P

NFFT = 256
NB = 127
BINS = 4
MODES = 4
ITERS = 8
MICS = 1024
SAMPLES = 16384
DEVICES = 128
LOCAL = 256
CHUNKS = SAMPLES // NFFT
PIECES = (20, 32, 12)
AHEAD = 2
PAIR = 2
AXES = ("wide", "narrow")
NT = (((1,), (1,)), ((), ()))
NN = (((1,), (0,)), ((), ()))
BF = jnp.bfloat16
F32 = jnp.float32


def split(x):
    hi = x.astype(BF)
    return hi, (x - hi.astype(F32)).astype(BF)


def dot(a, b, dims):
    return lax.dot_general(a, b, dims, preferred_element_type=F32)


def gram_kernel(
    starts_hbm, bins_hbm, weights_hbm, pressure_hbm, gram_ref, high_ref, low_ref,
    starts_ref, bins_ref, weights_ref, pressure_ref, rows_ref, q_ref, small_sems, sems,
):
    small = [
        pltpu.make_async_copy(starts_hbm, starts_ref, small_sems.at[0]),
        pltpu.make_async_copy(bins_hbm, bins_ref, small_sems.at[1]),
        pltpu.make_async_copy(weights_hbm, weights_ref, small_sems.at[2]),
    ]
    copies = []
    begin = 0
    for piece, chunks in enumerate(PIECES):
        rows = slice(begin * NFFT, (begin + chunks) * NFFT)
        copies.append(pltpu.make_async_copy(pressure_hbm.at[rows, :], pressure_ref.at[rows, :], sems.at[piece]))
        begin += chunks
    for copy in small:
        copy.start()
    for copy in copies[:AHEAD]:
        copy.start()

    row = lax.broadcasted_iota(jnp.int32, (8, NFFT), 0)
    time = lax.broadcasted_iota(jnp.int32, (8, NFFT), 1)
    which = row & 3
    window = 0.5 - 0.5 * jnp.cos(2.0 * math.pi * time.astype(F32) / NFFT)
    scaled = np.float32(1.0 / math.sqrt(0.375 * NFFT)) * window
    for copy in small:
        copy.wait()
    bins = jnp.where(
        which == 0,
        bins_ref[0],
        jnp.where(which == 1, bins_ref[1], jnp.where(which == 2, bins_ref[2], bins_ref[3])),
    )
    phase = 2.0 * math.pi * ((bins * time) & (NFFT - 1)).astype(F32) / NFFT
    table = jnp.where(row < 4, scaled * jnp.cos(phase), -scaled * jnp.sin(phase))
    table = table.astype(BF).astype(F32)
    zero = jnp.zeros((8, NFFT), F32)

    rolled = {}
    for c in range(CHUNKS):
        parts = []
        for block in range(2 * c - 2, 2 * c + 3):
            if block < 0 or block >= NB:
                parts.append(zero)
                continue
            start = starts_ref[block]
            if block not in rolled:
                rolled[block] = pltpu.roll(table, start & (NFFT - 1), 1)
            at = time + (c * NFFT - start)
            parts.append(jnp.where((at >= 0) & (at < NFFT), rolled[block], 0.0))
        parts.append(zero)
        rows_ref[c] = jnp.concatenate(parts, 0).astype(BF)

    sums = {}
    begin = 0
    for piece, chunks in enumerate(PIECES):
        copies[piece].wait()
        if piece + AHEAD < len(PIECES):
            copies[piece + AHEAD].start()
        for c in range(begin, begin + chunks):
            got = dot(rows_ref[c], pressure_ref[c * NFFT : (c + 1) * NFFT, :], NN)
            for k, block in enumerate(range(2 * c - 2, 2 * c + 3)):
                if 0 <= block < NB:
                    part = got[8 * k : 8 * k + 8]
                    sums[block] = sums[block] + part if block in sums else part
            for block in sorted(sums):
                if block <= 2 * c - 1 or c == CHUNKS - 1:
                    done = sums.pop(block)
                    q_ref[0, 8 * block : 8 * block + 8, :] = done[:, :128]
                    q_ref[1, 8 * block : 8 * block + 8, :] = done[:, 128:]
        begin += chunks
    for h in range(2):
        q_ref[h, 8 * NB : 8 * NB + 8, :] = jnp.zeros((8, 128), F32)

    weights = weights_ref[...]
    upper = lax.broadcasted_iota(jnp.int32, (128, 128), 1) >= lax.broadcasted_iota(jnp.int32, (128, 128), 0)
    for f in range(BINS):
        halves = [
            jnp.concatenate([q_ref[h, pl.ds(g, 128, stride=8), :] for g in (f, 4 + f)], 0) for h in range(2)
        ]
        both = jnp.concatenate(halves, 1)
        hi, lo = split(both)
        high_ref[f] = hi
        low_ref[f] = lo
        whi, wlo = split(both * weights)
        prod = dot(whi, hi, NT) + dot(wlo, hi, NT) + dot(whi, lo, NT)
        gram_re = prod[:128, :128] + prod[128:, 128:]
        gram_im = prod[:128, 128:] - prod[128:, :128]
        gram_ref[f * 128 : (f + 1) * 128, :] = jnp.where(upper, gram_re, gram_im)


def in_hbm(x):
    return pltpu.with_memory_space_constraint(x, pltpu.HBM)


def local_gram(pressure, weights, starts, bin_index):
    hbm = pl.BlockSpec(memory_space=pltpu.HBM)
    return pl.pallas_call(
        gram_kernel,
        out_shape=(
            jax.ShapeDtypeStruct((BINS * 128, 128), F32),
            jax.ShapeDtypeStruct((BINS, 256, LOCAL), BF),
            jax.ShapeDtypeStruct((BINS, 256, LOCAL), BF),
        ),
        in_specs=[hbm] * 4,
        scratch_shapes=[
            pltpu.SMEM((NB,), jnp.int32),
            pltpu.SMEM((BINS,), jnp.int32),
            pltpu.VMEM((1, LOCAL), F32),
            pltpu.VMEM((SAMPLES, LOCAL), BF),
            pltpu.VMEM((CHUNKS, 48, NFFT), BF),
            pltpu.VMEM((2, 1024, 128), F32),
            pltpu.SemaphoreType.DMA((3,)),
            pltpu.SemaphoreType.DMA((len(PIECES),)),
        ],
        compiler_params=pltpu.CompilerParams(vmem_limit_bytes=24 << 20),
        cost_estimate=pl.CostEstimate(flops=800_000_000, transcendentals=0, bytes_accessed=10_000_000),
        name="gram",
    )(in_hbm(starts), in_hbm(bin_index), in_hbm(weights.reshape(1, LOCAL)), in_hbm(pressure))


def project_kernel(left_ref, right_ref, high_ref, low_ref, phigh_ref, plow_ref):
    hi = high_ref[0]
    lo = low_ref[0]
    for tile in range(4):
        cols = slice(tile * 256, (tile + 1) * 256)
        parts = []
        for side in range(2):
            halves = [
                jnp.concatenate([ref[0, side, pl.ds(2 * tile + i, 128, stride=8), :] for i in range(2)], 0)
                for ref in (left_ref, right_ref)
            ]
            mics = jnp.concatenate(halves, 1)
            ghi, glo = split(mics)
            parts.append(dot(hi, ghi, NT) + dot(lo, ghi, NT) + dot(hi, glo, NT))
        by_re, by_im = parts
        phi, plo = split(by_re[:128] - by_im[128:])
        phigh_ref[0, :128, cols] = phi
        plow_ref[0, :128, cols] = plo
        phi, plo = split(by_re[128:] + by_im[:128])
        phigh_ref[0, 128:, cols] = phi
        plow_ref[0, 128:, cols] = plo


def project(green_table, high, low, first):
    return pl.pallas_call(
        project_kernel,
        out_shape=(
            pltpu.HBM((PAIR, 256, MICS), BF),
            pltpu.HBM((PAIR, 256, MICS), BF),
        ),
        grid=(PAIR,),
        in_specs=[
            pl.BlockSpec((1, 2, MICS, 128), lambda f: (first + f, 0, 0, 0)),
            pl.BlockSpec((1, 2, MICS, 128), lambda f: (first + f, 0, 0, 1)),
            pl.BlockSpec((1, 256, LOCAL), lambda f: (first + f, 0, 0)),
            pl.BlockSpec((1, 256, LOCAL), lambda f: (first + f, 0, 0)),
        ],
        out_specs=[
            pl.BlockSpec((1, 256, MICS), lambda f: (f, 0, 0)),
            pl.BlockSpec((1, 256, MICS), lambda f: (f, 0, 0)),
        ],
        compiler_params=pltpu.CompilerParams(vmem_limit_bytes=24 << 20),
        cost_estimate=pl.CostEstimate(flops=1_650_000_000, transcendentals=0, bytes_accessed=7_000_000),
        name="project",
    )(in_hbm(green_table), in_hbm(green_table), high, low)


def share_kernel(parts_ref, out_ref):
    total = parts_ref[0:8, :]
    for s in range(1, 64):
        total = total + parts_ref[8 * s : 8 * s + 8, :]
    total = total + pltpu.roll(total, 4, 0)
    for s in range(64):
        out_ref[8 * s : 8 * s + 8, :] = total


def share_sum(parts):
    return pl.pallas_call(
        share_kernel,
        out_shape=jax.ShapeDtypeStruct((512, 128), F32),
        compiler_params=pltpu.CompilerParams(vmem_limit_bytes=4 << 20),
        name="share",
    )(parts)


def modes_kernel(gram_ref, start_ref, high01, low01, high23, low23, out_ref, phigh_ref, plow_ref, sems):
    fetch = []
    for pair, (high, low) in enumerate(((high01, low01), (high23, low23))):
        place = slice(PAIR * pair, PAIR * pair + PAIR)
        fetch.append(pltpu.make_async_copy(high, phigh_ref.at[place], sems.at[2 * pair]))
        fetch.append(pltpu.make_async_copy(low, plow_ref.at[place], sems.at[2 * pair + 1]))
    for copy in fetch:
        copy.start()
    col = lax.broadcasted_iota(jnp.int32, (128, 128), 1)
    row = lax.broadcasted_iota(jnp.int32, (128, 128), 0)
    lane_row = lax.broadcasted_iota(jnp.int32, (8, 128), 0)
    sign = jnp.where(lane_row < 4, 1.0, -1.0)
    mats = []
    for f in range(BINS):
        packed = gram_ref[f * 128 : (f + 1) * 128, :]
        flipped = packed.T
        gram_re = jnp.where(col >= row, packed, flipped)
        gram_im = jnp.where(col < row, packed, jnp.where(col > row, -flipped, 0.0))
        mats.append(split(jnp.concatenate([gram_re, gram_im], 1)))
    vecs = [start_ref[...]] * BINS
    for _ in range(ITERS):
        images = []
        for f in range(BINS):
            hi, lo = split(vecs[f])
            ghi, glo = mats[f]
            stacked = jnp.concatenate([hi, lo], 0)
            prod = dot(stacked, ghi, NN)
            prod = prod[:8] + prod[8:] + dot(hi, glo, NN)
            swapped = pltpu.roll(prod[:, 128:], 4, 0)
            images.append(prod[:, :128] + sign * swapped)
        for j in range(MODES):
            for f in range(BINS):
                y = images[f]
                vre = y[j : j + 1, :]
                vim = y[4 + j : 5 + j, :]
                turned = sign * pltpu.roll(y, 4, 0)
                coef = jnp.sum(y * vre + turned * vim, axis=1, keepdims=True)
                inverse = lax.rsqrt(coef[j : j + 1, :] + 1e-06)
                coef = jnp.broadcast_to(coef, (8, 128))
                scaled = coef * (inverse * inverse)
                cross = -sign * pltpu.roll(scaled, 4, 0)
                later = (lane_row & 3) > j
                here = (lane_row & 3) == j
                left = y - (scaled * vre + cross * vim)
                images[f] = jnp.where(later, left, jnp.where(here, y * inverse, y))
        vecs = images
    for copy in fetch:
        copy.wait()
    amps = []
    for f in range(BINS):
        y = vecs[f]
        turned = -sign * pltpu.roll(y, 4, 0)
        hi, lo = split(jnp.concatenate([y, turned], 1))
        prod = dot(jnp.concatenate([hi, lo], 0), phigh_ref[f], NN)
        amps.append(prod[:8] + prod[8:] + dot(hi, plow_ref[f], NN))
    for half in range(2):
        rows = []
        for i in range(4 * half, 4 * half + 4):
            for f in range(BINS):
                rows.append(amps[f][:, i * 128 : (i + 1) * 128])
        out_ref[pl.ds(half, 128, stride=2), :] = jnp.concatenate(rows, 0).T


def start_basis():
    rowpos = np.arange(NB) + 0.5
    colpos = np.arange(MODES) + 1.0
    basis = np.zeros((8, 128), np.float32)
    basis[:MODES, :NB] = np.cos(math.pi * colpos[:, None] * rowpos[None, :] / NB)
    return jnp.asarray(basis)


def amplitudes(gram, projected):
    return pl.pallas_call(
        modes_kernel,
        out_shape=jax.ShapeDtypeStruct((2 * DEVICES, 128), F32),
        in_specs=[pl.BlockSpec(memory_space=pltpu.VMEM)] * 2 + [pl.BlockSpec(memory_space=pltpu.HBM)] * 4,
        scratch_shapes=[
            pltpu.VMEM((BINS, 256, MICS), BF),
            pltpu.VMEM((BINS, 256, MICS), BF),
            pltpu.SemaphoreType.DMA((4,)),
        ],
        compiler_params=pltpu.CompilerParams(vmem_limit_bytes=24 << 20),
        name="modes",
    )(gram, start_basis(), *[in_hbm(x) for x in projected])


def power_kernel(parts_ref, out_ref):
    total = parts_ref[0:8, :]
    for s in range(1, 32):
        total = total + parts_ref[8 * s : 8 * s + 8, :]
    total = total + pltpu.roll(total, 4, 0)
    total = total + pltpu.roll(total, 6, 0)
    square = total * total
    lane = lax.broadcasted_iota(jnp.int32, (8, 128), 1)
    row = lax.broadcasted_iota(jnp.int32, (8, 128), 0)
    mic = lax.broadcasted_iota(jnp.int32, (8, 8), 1)
    out = jnp.zeros((8, 8), F32)
    for half in range(2):
        source = jnp.broadcast_to(square[half : half + 1, :], (8, 128))
        for i in range(4):
            sums = jnp.sum(jnp.where((lane >> 3) == 4 * i + row, source, 0.0), axis=1, keepdims=True)
            out = jnp.where(mic == 4 * half + i, sums, out)
    out_ref[...] = out[:BINS, :]


def power(parts):
    return pl.pallas_call(
        power_kernel,
        out_shape=jax.ShapeDtypeStruct((BINS, MICS // DEVICES), F32),
        compiler_params=pltpu.CompilerParams(vmem_limit_bytes=4 << 20),
        name="power",
    )(parts).T


def exchange(x):
    return lax.all_to_all(x, AXES, 0, 0, tiled=True)


def on_device(pressure, weights, green_table, starts, bin_index):
    gram, high, low = local_gram(pressure, weights, starts, bin_index)
    parts = exchange(gram.reshape(DEVICES, 4, 128))
    early = project(green_table, high, low, 0)
    parts, early = lax.optimization_barrier((parts, early))
    shared = share_sum(parts.reshape(512, 128))
    shared, high, low = lax.optimization_barrier((shared, high, low))
    summed = exchange(shared.reshape(DEVICES, 4, 128)).reshape(512, 128)
    late = project(green_table, high, low, PAIR)
    partial = amplitudes(summed, (*early, *late))
    return power(exchange(partial.reshape(DEVICES, 2, 128)).reshape(2 * DEVICES, 128))


def solution(mesh):
    return jax.shard_map(
        on_device,
        mesh=mesh,
        in_specs=(
            P(None, AXES),
            P(AXES),
            P(None, None, None, AXES),
            P(),
            P(),
        ),
        out_specs=P(AXES, None),
        check_vma=False,
    )
```

```python
import math

import jax
import jax.numpy as jnp
import numpy as np
from jax import lax
from jax.experimental import pallas as pl
from jax.experimental.pallas import tpu as pltpu
from jax.sharding import PartitionSpec as P

NFFT = 256
NB = 127
BINS = 4
MODES = 4
ITERS = 8
KEPT = 0.01
MICS = 1024
SAMPLES = 16384
DEVICES = 128
LOCAL = 256
CHUNKS = SAMPLES // NFFT
PIECES = (20, 32, 12)
AHEAD = 2
PAIR = 2
AXES = ("wide", "narrow")
NT = (((1,), (1,)), ((), ()))
NN = (((1,), (0,)), ((), ()))
BF = jnp.bfloat16
F32 = jnp.float32


def split(x):
    hi = x.astype(BF)
    return hi, (x - hi.astype(F32)).astype(BF)


def dot(a, b, dims):
    return lax.dot_general(a, b, dims, preferred_element_type=F32)


def gram_kernel(
    starts_hbm, bins_hbm, weights_hbm, pressure_hbm, gram_ref, high_ref, low_ref,
    starts_ref, bins_ref, weights_ref, pressure_ref, rows_ref, q_ref, small_sems, sems,
):
    small = [
        pltpu.make_async_copy(starts_hbm, starts_ref, small_sems.at[0]),
        pltpu.make_async_copy(bins_hbm, bins_ref, small_sems.at[1]),
        pltpu.make_async_copy(weights_hbm, weights_ref, small_sems.at[2]),
    ]
    copies = []
    begin = 0
    for piece, chunks in enumerate(PIECES):
        rows = slice(begin * NFFT, (begin + chunks) * NFFT)
        copies.append(pltpu.make_async_copy(pressure_hbm.at[rows, :], pressure_ref.at[rows, :], sems.at[piece]))
        begin += chunks
    for copy in small:
        copy.start()
    for copy in copies[:AHEAD]:
        copy.start()

    row = lax.broadcasted_iota(jnp.int32, (8, NFFT), 0)
    time = lax.broadcasted_iota(jnp.int32, (8, NFFT), 1)
    which = row & 3
    window = 0.5 - 0.5 * jnp.cos(2.0 * math.pi * time.astype(F32) / NFFT)
    scaled = np.float32(1.0 / math.sqrt(0.375 * NFFT)) * window
    for copy in small:
        copy.wait()
    bins = jnp.where(
        which == 0,
        bins_ref[0],
        jnp.where(which == 1, bins_ref[1], jnp.where(which == 2, bins_ref[2], bins_ref[3])),
    )
    phase = 2.0 * math.pi * ((bins * time) & (NFFT - 1)).astype(F32) / NFFT
    table = jnp.where(row < 4, scaled * jnp.cos(phase), -scaled * jnp.sin(phase))
    table = table.astype(BF).astype(F32)
    zero = jnp.zeros((8, NFFT), F32)

    rolled = {}
    for c in range(CHUNKS):
        parts = []
        for block in range(2 * c - 2, 2 * c + 3):
            if block < 0 or block >= NB:
                parts.append(zero)
                continue
            start = starts_ref[block]
            if block not in rolled:
                rolled[block] = pltpu.roll(table, start & (NFFT - 1), 1)
            at = time + (c * NFFT - start)
            parts.append(jnp.where((at >= 0) & (at < NFFT), rolled[block], 0.0))
        parts.append(zero)
        rows_ref[c] = jnp.concatenate(parts, 0).astype(BF)

    sums = {}
    begin = 0
    for piece, chunks in enumerate(PIECES):
        copies[piece].wait()
        if piece + AHEAD < len(PIECES):
            copies[piece + AHEAD].start()
        for c in range(begin, begin + chunks):
            got = dot(rows_ref[c], pressure_ref[c * NFFT : (c + 1) * NFFT, :], NN)
            for k, block in enumerate(range(2 * c - 2, 2 * c + 3)):
                if 0 <= block < NB:
                    part = got[8 * k : 8 * k + 8]
                    sums[block] = sums[block] + part if block in sums else part
            for block in sorted(sums):
                if block <= 2 * c - 1 or c == CHUNKS - 1:
                    done = sums.pop(block)
                    q_ref[0, 8 * block : 8 * block + 8, :] = done[:, :128]
                    q_ref[1, 8 * block : 8 * block + 8, :] = done[:, 128:]
        begin += chunks
    for h in range(2):
        q_ref[h, 8 * NB : 8 * NB + 8, :] = jnp.zeros((8, 128), F32)

    weights = weights_ref[...]
    upper = lax.broadcasted_iota(jnp.int32, (128, 128), 1) >= lax.broadcasted_iota(jnp.int32, (128, 128), 0)
    for f in range(BINS):
        halves = [
            jnp.concatenate([q_ref[h, pl.ds(g, 128, stride=8), :] for g in (f, 4 + f)], 0) for h in range(2)
        ]
        both = jnp.concatenate(halves, 1)
        hi, lo = split(both)
        high_ref[f] = hi
        low_ref[f] = lo
        whi, wlo = split(both * weights)
        prod = dot(whi, hi, NT) + dot(wlo, hi, NT) + dot(whi, lo, NT)
        gram_re = prod[:128, :128] + prod[128:, 128:]
        gram_im = prod[:128, 128:] - prod[128:, :128]
        gram_ref[f * 128 : (f + 1) * 128, :] = jnp.where(upper, gram_re, gram_im)


def in_hbm(x):
    return pltpu.with_memory_space_constraint(x, pltpu.HBM)


def local_gram(pressure, weights, starts, bin_index):
    hbm = pl.BlockSpec(memory_space=pltpu.HBM)
    return pl.pallas_call(
        gram_kernel,
        out_shape=(
            jax.ShapeDtypeStruct((BINS * 128, 128), F32),
            jax.ShapeDtypeStruct((BINS, 256, LOCAL), BF),
            jax.ShapeDtypeStruct((BINS, 256, LOCAL), BF),
        ),
        in_specs=[hbm] * 4,
        scratch_shapes=[
            pltpu.SMEM((NB,), jnp.int32),
            pltpu.SMEM((BINS,), jnp.int32),
            pltpu.VMEM((1, LOCAL), F32),
            pltpu.VMEM((SAMPLES, LOCAL), BF),
            pltpu.VMEM((CHUNKS, 48, NFFT), BF),
            pltpu.VMEM((2, 1024, 128), F32),
            pltpu.SemaphoreType.DMA((3,)),
            pltpu.SemaphoreType.DMA((len(PIECES),)),
        ],
        compiler_params=pltpu.CompilerParams(vmem_limit_bytes=24 << 20),
        cost_estimate=pl.CostEstimate(flops=800_000_000, transcendentals=0, bytes_accessed=10_000_000),
        name="gram",
    )(in_hbm(starts), in_hbm(bin_index), in_hbm(weights.reshape(1, LOCAL)), in_hbm(pressure))


def project_kernel(left_ref, right_ref, high_ref, low_ref, phigh_ref, plow_ref):
    hi = high_ref[0]
    lo = low_ref[0]
    for tile in range(4):
        cols = slice(tile * 256, (tile + 1) * 256)
        parts = []
        for side in range(2):
            halves = [
                jnp.concatenate([ref[0, side, pl.ds(2 * tile + i, 128, stride=8), :] for i in range(2)], 0)
                for ref in (left_ref, right_ref)
            ]
            mics = jnp.concatenate(halves, 1)
            ghi, glo = split(mics)
            parts.append(dot(hi, ghi, NT) + dot(lo, ghi, NT) + dot(hi, glo, NT))
        by_re, by_im = parts
        phi, plo = split(by_re[:128] - by_im[128:])
        phigh_ref[0, :128, cols] = phi
        plow_ref[0, :128, cols] = plo
        phi, plo = split(by_re[128:] + by_im[:128])
        phigh_ref[0, 128:, cols] = phi
        plow_ref[0, 128:, cols] = plo


def project(green_table, high, low, first):
    return pl.pallas_call(
        project_kernel,
        out_shape=(
            pltpu.HBM((PAIR, 256, MICS), BF),
            pltpu.HBM((PAIR, 256, MICS), BF),
        ),
        grid=(PAIR,),
        in_specs=[
            pl.BlockSpec((1, 2, MICS, 128), lambda f: (first + f, 0, 0, 0)),
            pl.BlockSpec((1, 2, MICS, 128), lambda f: (first + f, 0, 0, 1)),
            pl.BlockSpec((1, 256, LOCAL), lambda f: (first + f, 0, 0)),
            pl.BlockSpec((1, 256, LOCAL), lambda f: (first + f, 0, 0)),
        ],
        out_specs=[
            pl.BlockSpec((1, 256, MICS), lambda f: (f, 0, 0)),
            pl.BlockSpec((1, 256, MICS), lambda f: (f, 0, 0)),
        ],
        compiler_params=pltpu.CompilerParams(vmem_limit_bytes=24 << 20),
        cost_estimate=pl.CostEstimate(flops=1_650_000_000, transcendentals=0, bytes_accessed=7_000_000),
        name="project",
    )(in_hbm(green_table), in_hbm(green_table), high, low)


def share_kernel(parts_ref, out_ref):
    total = parts_ref[0:8, :]
    for s in range(1, 64):
        total = total + parts_ref[8 * s : 8 * s + 8, :]
    total = total + pltpu.roll(total, 4, 0)
    for s in range(64):
        out_ref[8 * s : 8 * s + 8, :] = total


def share_sum(parts):
    return pl.pallas_call(
        share_kernel,
        out_shape=jax.ShapeDtypeStruct((512, 128), F32),
        compiler_params=pltpu.CompilerParams(vmem_limit_bytes=4 << 20),
        name="share",
    )(parts)


def row(x, index):
    return jnp.broadcast_to(x[index : index + 1, :], (8, 128))


def lane_sum(x):
    return jnp.broadcast_to(jnp.sum(x, axis=1, keepdims=True), (8, 128))


def by_columns(y, turned, later, here):
    for j in range(MODES):
        vre, vim = row(y, j), row(y, 4 + j)
        inverse = lax.rsqrt(lane_sum(vre * vre + vim * vim) + 1e-06)
        scale = inverse if j == 0 else jnp.where(here[j], inverse, scale)
        if j < MODES - 1:
            square = jnp.where(later[j], inverse * inverse, 0.0)
            coef = lane_sum(y * vre + turned * vim) * square
            cross = lane_sum(y * vim - turned * vre) * square
            y, turned = y - (coef * vre + cross * vim), turned - (coef * vim - cross * vre)
    return (y, turned), scale


def by_products(y, turned, later, here):
    coefs, crosses = [], []
    for j in range(MODES):
        vre, vim = row(y, j), row(y, 4 + j)
        coefs.append(lane_sum(y * vre + turned * vim))
        crosses.append(lane_sum(y * vim - turned * vre) if j < MODES - 1 else None)
    whole = [row(coefs[j], j) * KEPT for j in range(MODES)]
    sound = None
    for j in range(MODES):
        norm = row(coefs[j], j)
        kept = jnp.where(norm >= whole[j], 1.0, 0.0)
        sound = kept if j == 0 else jnp.minimum(sound, kept)
        inverse = lax.rsqrt(norm + 1e-06)
        scale = inverse if j == 0 else jnp.where(here[j], inverse, scale)
        if j < MODES - 1:
            square = inverse * inverse
            twice = square * (2.0 - square * norm)
            coef, cross = coefs[j], crosses[j]
            for i in range(j + 1, MODES):
                are, aim = row(coef, i) * twice, row(coef, 4 + i) * twice
                coefs[i] = coefs[i] - (are * coef - aim * cross)
                if i < MODES - 1:
                    crosses[i] = crosses[i] - (are * cross + aim * coef)
            square = jnp.where(later[j], square, 0.0)
            coef, cross = coef * square, cross * square
            vre, vim = row(y, j), row(y, 4 + j)
            y, turned = y - (coef * vre + cross * vim), turned - (coef * vim - cross * vre)
    return (y, turned), scale, sound


def modes_kernel(gram_ref, start_ref, high01, low01, high23, low23, out_ref, phigh_ref, plow_ref, mats_ref, sems):
    fetch = []
    for pair, (high, low) in enumerate(((high01, low01), (high23, low23))):
        place = slice(PAIR * pair, PAIR * pair + PAIR)
        fetch.append(pltpu.make_async_copy(high, phigh_ref.at[place], sems.at[2 * pair]))
        fetch.append(pltpu.make_async_copy(low, plow_ref.at[place], sems.at[2 * pair + 1]))
    for copy in fetch:
        copy.start()
    col = lax.broadcasted_iota(jnp.int32, (128, 128), 1)
    row = lax.broadcasted_iota(jnp.int32, (128, 128), 0)
    lane_row = lax.broadcasted_iota(jnp.int32, (8, 128), 0)
    sign = jnp.where(lane_row < 4, 1.0, -1.0)
    mode = lane_row & 3
    later = [mode > j for j in range(MODES)]
    here = [mode == j for j in range(MODES)]
    for f in range(BINS):
        packed = gram_ref[f * 128 : (f + 1) * 128, :]
        flipped = packed.T
        gram_re = jnp.where(col >= row, packed, flipped)
        gram_im = jnp.where(col < row, packed, jnp.where(col > row, -flipped, 0.0))
        mats_ref[f, 0], mats_ref[f, 1] = split(jnp.concatenate([gram_re, gram_im], 0))
    start = start_ref[...]

    def iterate(fast):
        vecs = [(start, sign * pltpu.roll(start, 4, 0))] * BINS
        sound = jnp.ones((8, 128), F32)
        for _ in range(ITERS):
            pairs = []
            for f in range(BINS):
                hi, lo = split(jnp.concatenate(vecs[f], 1))
                ghi, glo = mats_ref[f, 0], mats_ref[f, 1]
                prod = dot(jnp.concatenate([hi, lo], 0), ghi, NN)
                image = prod[:8] + prod[8:] + dot(hi, glo, NN)
                pairs.append((image, sign * pltpu.roll(image, 4, 0)))
            vecs = []
            for f in range(BINS):
                if fast:
                    (y, turned), scale, kept = by_products(*pairs[f], later, here)
                    sound = jnp.minimum(sound, kept)
                else:
                    (y, turned), scale = by_columns(*pairs[f], later, here)
                vecs.append((y * scale, turned * scale))
        return vecs, sound

    def finish(vecs):
        amps = []
        for f in range(BINS):
            y, turned = vecs[f]
            hi, lo = split(jnp.concatenate([y, -turned], 1))
            prod = dot(jnp.concatenate([hi, lo], 0), phigh_ref[f], NN)
            amps.append(prod[:8] + prod[8:] + dot(hi, plow_ref[f], NN))
        for half in range(2):
            rows = []
            for i in range(4 * half, 4 * half + 4):
                for f in range(BINS):
                    rows.append(amps[f][:, i * 128 : (i + 1) * 128])
            out_ref[pl.ds(half, 128, stride=2), :] = jnp.concatenate(rows, 0).T

    vecs, sound = iterate(True)
    is_sound = jnp.min(sound) > 0.5
    for copy in fetch:
        copy.wait()
    finish(vecs)

    @pl.when(jnp.logical_not(is_sound))
    def _():
        finish(iterate(False)[0])


def start_basis():
    rowpos = np.arange(NB) + 0.5
    colpos = np.arange(MODES) + 1.0
    basis = np.zeros((8, 128), np.float32)
    basis[:MODES, :NB] = np.cos(math.pi * colpos[:, None] * rowpos[None, :] / NB)
    return jnp.asarray(basis)


def amplitudes(gram, projected):
    return pl.pallas_call(
        modes_kernel,
        out_shape=jax.ShapeDtypeStruct((2 * DEVICES, 128), F32),
        in_specs=[pl.BlockSpec(memory_space=pltpu.VMEM)] * 2 + [pl.BlockSpec(memory_space=pltpu.HBM)] * 4,
        scratch_shapes=[
            pltpu.VMEM((BINS, 256, MICS), BF),
            pltpu.VMEM((BINS, 256, MICS), BF),
            pltpu.VMEM((BINS, 2, 256, 128), BF),
            pltpu.SemaphoreType.DMA((4,)),
        ],
        compiler_params=pltpu.CompilerParams(vmem_limit_bytes=24 << 20),
        name="modes",
    )(gram, start_basis(), *[in_hbm(x) for x in projected])


def power_kernel(parts_ref, out_ref):
    total = parts_ref[0:8, :]
    for s in range(1, 32):
        total = total + parts_ref[8 * s : 8 * s + 8, :]
    total = total + pltpu.roll(total, 4, 0)
    total = total + pltpu.roll(total, 6, 0)
    square = total * total
    lane = lax.broadcasted_iota(jnp.int32, (8, 128), 1)
    row = lax.broadcasted_iota(jnp.int32, (8, 128), 0)
    mic = lax.broadcasted_iota(jnp.int32, (8, 8), 1)
    out = jnp.zeros((8, 8), F32)
    for half in range(2):
        source = jnp.broadcast_to(square[half : half + 1, :], (8, 128))
        for i in range(4):
            sums = jnp.sum(jnp.where((lane >> 3) == 4 * i + row, source, 0.0), axis=1, keepdims=True)
            out = jnp.where(mic == 4 * half + i, sums, out)
    out_ref[...] = out[:BINS, :]


def power(parts):
    return pl.pallas_call(
        power_kernel,
        out_shape=jax.ShapeDtypeStruct((BINS, MICS // DEVICES), F32),
        compiler_params=pltpu.CompilerParams(vmem_limit_bytes=4 << 20),
        name="power",
    )(parts).T


def exchange(x):
    return lax.all_to_all(x, AXES, 0, 0, tiled=True)


def on_device(pressure, weights, green_table, starts, bin_index):
    gram, high, low = local_gram(pressure, weights, starts, bin_index)
    parts = exchange(gram.reshape(DEVICES, 4, 128))
    early = project(green_table, high, low, 0)
    parts, early = lax.optimization_barrier((parts, early))
    shared = share_sum(parts.reshape(512, 128))
    shared, high, low = lax.optimization_barrier((shared, high, low))
    summed = exchange(shared.reshape(DEVICES, 4, 128)).reshape(512, 128)
    late = project(green_table, high, low, PAIR)
    partial = amplitudes(summed, (*early, *late))
    return power(exchange(partial.reshape(DEVICES, 2, 128)).reshape(2 * DEVICES, 128))


def solution(mesh):
    return jax.shard_map(
        on_device,
        mesh=mesh,
        in_specs=(
            P(None, AXES),
            P(AXES),
            P(None, None, None, AXES),
            P(),
            P(),
        ),
        out_specs=P(AXES, None),
        check_vma=False,
    )
```

```python
import math

import jax
import jax.numpy as jnp
import numpy as np
from jax import lax
from jax.experimental import pallas as pl
from jax.experimental.pallas import tpu as pltpu
from jax.sharding import PartitionSpec as P

NFFT = 256
NB = 127
BINS = 4
MODES = 4
ITERS = 8
KEPT = 0.01
MICS = 1024
SAMPLES = 16384
DEVICES = 128
LOCAL = 256
CHUNKS = SAMPLES // NFFT
PIECES = (20, 32, 12)
AHEAD = 2
PAIR = 2
AXES = ("wide", "narrow")
NT = (((1,), (1,)), ((), ()))
NN = (((1,), (0,)), ((), ()))
BF = jnp.bfloat16
F32 = jnp.float32


def split(x):
    hi = x.astype(BF)
    return hi, (x - hi.astype(F32)).astype(BF)


def dot(a, b, dims):
    return lax.dot_general(a, b, dims, preferred_element_type=F32)


def gram_kernel(
    starts_hbm, bins_hbm, weights_hbm, pressure_hbm, gram_ref, high_ref, low_ref,
    starts_ref, bins_ref, weights_ref, pressure_ref, rows_ref, q_ref, small_sems, sems,
):
    small = [
        pltpu.make_async_copy(starts_hbm, starts_ref, small_sems.at[0]),
        pltpu.make_async_copy(bins_hbm, bins_ref, small_sems.at[1]),
        pltpu.make_async_copy(weights_hbm, weights_ref, small_sems.at[2]),
    ]
    copies = []
    begin = 0
    for piece, chunks in enumerate(PIECES):
        rows = slice(begin * NFFT, (begin + chunks) * NFFT)
        copies.append(pltpu.make_async_copy(pressure_hbm.at[rows, :], pressure_ref.at[rows, :], sems.at[piece]))
        begin += chunks
    for copy in small:
        copy.start()
    for copy in copies[:AHEAD]:
        copy.start()

    row = lax.broadcasted_iota(jnp.int32, (8, NFFT), 0)
    time = lax.broadcasted_iota(jnp.int32, (8, NFFT), 1)
    which = row & 3
    window = 0.5 - 0.5 * jnp.cos(2.0 * math.pi * time.astype(F32) / NFFT)
    scaled = np.float32(1.0 / math.sqrt(0.375 * NFFT)) * window
    for copy in small:
        copy.wait()
    bins = jnp.where(
        which == 0,
        bins_ref[0],
        jnp.where(which == 1, bins_ref[1], jnp.where(which == 2, bins_ref[2], bins_ref[3])),
    )
    phase = 2.0 * math.pi * ((bins * time) & (NFFT - 1)).astype(F32) / NFFT
    table = jnp.where(row < 4, scaled * jnp.cos(phase), -scaled * jnp.sin(phase))
    table = table.astype(BF).astype(F32)
    zero = jnp.zeros((8, NFFT), F32)

    rolled = {}
    for c in range(CHUNKS):
        parts = []
        for block in range(2 * c - 2, 2 * c + 3):
            if block < 0 or block >= NB:
                parts.append(zero)
                continue
            start = starts_ref[block]
            if block not in rolled:
                rolled[block] = pltpu.roll(table, start & (NFFT - 1), 1)
            at = time + (c * NFFT - start)
            parts.append(jnp.where((at >= 0) & (at < NFFT), rolled[block], 0.0))
        parts.append(zero)
        rows_ref[c] = jnp.concatenate(parts, 0).astype(BF)

    sums = {}
    begin = 0
    for piece, chunks in enumerate(PIECES):
        copies[piece].wait()
        if piece + AHEAD < len(PIECES):
            copies[piece + AHEAD].start()
        for c in range(begin, begin + chunks):
            got = dot(rows_ref[c], pressure_ref[c * NFFT : (c + 1) * NFFT, :], NN)
            for k, block in enumerate(range(2 * c - 2, 2 * c + 3)):
                if 0 <= block < NB:
                    part = got[8 * k : 8 * k + 8]
                    sums[block] = sums[block] + part if block in sums else part
            for block in sorted(sums):
                if block <= 2 * c - 1 or c == CHUNKS - 1:
                    done = sums.pop(block)
                    q_ref[0, 8 * block : 8 * block + 8, :] = done[:, :128]
                    q_ref[1, 8 * block : 8 * block + 8, :] = done[:, 128:]
        begin += chunks
    for h in range(2):
        q_ref[h, 8 * NB : 8 * NB + 8, :] = jnp.zeros((8, 128), F32)

    weights = weights_ref[...]
    upper = lax.broadcasted_iota(jnp.int32, (128, 128), 1) >= lax.broadcasted_iota(jnp.int32, (128, 128), 0)
    for f in range(BINS):
        halves = [
            jnp.concatenate([q_ref[h, pl.ds(g, 128, stride=8), :] for g in (f, 4 + f)], 0) for h in range(2)
        ]
        both = jnp.concatenate(halves, 1)
        hi, lo = split(both)
        high_ref[f] = hi
        low_ref[f] = lo
        whi, wlo = split(both * weights)
        prod = dot(whi, hi, NT) + dot(wlo, hi, NT) + dot(whi, lo, NT)
        gram_re = prod[:128, :128] + prod[128:, 128:]
        gram_im = prod[:128, 128:] - prod[128:, :128]
        gram_ref[f * 128 : (f + 1) * 128, :] = jnp.where(upper, gram_re, gram_im)


def in_hbm(x):
    return pltpu.with_memory_space_constraint(x, pltpu.HBM)


def local_gram(pressure, weights, starts, bin_index):
    hbm = pl.BlockSpec(memory_space=pltpu.HBM)
    return pl.pallas_call(
        gram_kernel,
        out_shape=(
            jax.ShapeDtypeStruct((BINS * 128, 128), F32),
            jax.ShapeDtypeStruct((BINS, 256, LOCAL), BF),
            jax.ShapeDtypeStruct((BINS, 256, LOCAL), BF),
        ),
        in_specs=[hbm] * 4,
        scratch_shapes=[
            pltpu.SMEM((NB,), jnp.int32),
            pltpu.SMEM((BINS,), jnp.int32),
            pltpu.VMEM((1, LOCAL), F32),
            pltpu.VMEM((SAMPLES, LOCAL), BF),
            pltpu.VMEM((CHUNKS, 48, NFFT), BF),
            pltpu.VMEM((2, 1024, 128), F32),
            pltpu.SemaphoreType.DMA((3,)),
            pltpu.SemaphoreType.DMA((len(PIECES),)),
        ],
        compiler_params=pltpu.CompilerParams(vmem_limit_bytes=24 << 20),
        cost_estimate=pl.CostEstimate(flops=800_000_000, transcendentals=0, bytes_accessed=10_000_000),
        name="gram",
    )(in_hbm(starts), in_hbm(bin_index), in_hbm(weights.reshape(1, LOCAL)), in_hbm(pressure))


def project_kernel(left_ref, right_ref, high_ref, low_ref, phigh_ref, plow_ref):
    hi = high_ref[0]
    lo = low_ref[0]
    for tile in range(4):
        cols = slice(tile * 256, (tile + 1) * 256)
        parts = []
        for side in range(2):
            halves = [
                jnp.concatenate([ref[0, side, pl.ds(2 * tile + i, 128, stride=8), :] for i in range(2)], 0)
                for ref in (left_ref, right_ref)
            ]
            mics = jnp.concatenate(halves, 1)
            ghi, glo = split(mics)
            parts.append(dot(hi, ghi, NT) + dot(lo, ghi, NT) + dot(hi, glo, NT))
        by_re, by_im = parts
        phi, plo = split(by_re[:128] - by_im[128:])
        phigh_ref[0, :128, cols] = phi
        plow_ref[0, :128, cols] = plo
        phi, plo = split(by_re[128:] + by_im[:128])
        phigh_ref[0, 128:, cols] = phi
        plow_ref[0, 128:, cols] = plo


def project(green_table, high, low, first, shape):
    return pl.pallas_call(
        project_kernel,
        out_shape=(shape((PAIR, 256, MICS), BF), shape((PAIR, 256, MICS), BF)),
        grid=(PAIR,),
        in_specs=[
            pl.BlockSpec((1, 2, MICS, 128), lambda f: (first + f, 0, 0, 0)),
            pl.BlockSpec((1, 2, MICS, 128), lambda f: (first + f, 0, 0, 1)),
            pl.BlockSpec((1, 256, LOCAL), lambda f: (first + f, 0, 0)),
            pl.BlockSpec((1, 256, LOCAL), lambda f: (first + f, 0, 0)),
        ],
        out_specs=[
            pl.BlockSpec((1, 256, MICS), lambda f: (f, 0, 0)),
            pl.BlockSpec((1, 256, MICS), lambda f: (f, 0, 0)),
        ],
        compiler_params=pltpu.CompilerParams(vmem_limit_bytes=24 << 20),
        cost_estimate=pl.CostEstimate(flops=1_650_000_000, transcendentals=0, bytes_accessed=7_000_000),
        name="project",
    )(in_hbm(green_table), in_hbm(green_table), high, low)


def share_kernel(parts_ref, out_ref):
    total = parts_ref[0:8, :]
    for s in range(1, 64):
        total = total + parts_ref[8 * s : 8 * s + 8, :]
    total = total + pltpu.roll(total, 4, 0)
    for s in range(64):
        out_ref[8 * s : 8 * s + 8, :] = total


def share_sum(parts):
    return pl.pallas_call(
        share_kernel,
        out_shape=jax.ShapeDtypeStruct((512, 128), F32),
        compiler_params=pltpu.CompilerParams(vmem_limit_bytes=4 << 20),
        name="share",
    )(parts)


def row(x, index):
    return jnp.broadcast_to(x[index : index + 1, :], (8, 128))


def lane_sum(x):
    return jnp.broadcast_to(jnp.sum(x, axis=1, keepdims=True), (8, 128))


def by_columns(y, turned, later, here):
    for j in range(MODES):
        vre, vim = row(y, j), row(y, 4 + j)
        inverse = lax.rsqrt(lane_sum(vre * vre + vim * vim) + 1e-06)
        scale = inverse if j == 0 else jnp.where(here[j], inverse, scale)
        if j < MODES - 1:
            square = jnp.where(later[j], inverse * inverse, 0.0)
            coef = lane_sum(y * vre + turned * vim) * square
            cross = lane_sum(y * vim - turned * vre) * square
            y, turned = y - (coef * vre + cross * vim), turned - (coef * vim - cross * vre)
    return (y, turned), scale


def by_products(y, turned, later, here):
    coefs, crosses = [], []
    for j in range(MODES):
        vre, vim = row(y, j), row(y, 4 + j)
        coefs.append(lane_sum(y * vre + turned * vim))
        crosses.append(lane_sum(y * vim - turned * vre) if j < MODES - 1 else None)
    whole = [row(coefs[j], j) * KEPT for j in range(MODES)]
    steps = []
    for j in range(MODES):
        norm = row(coefs[j], j)
        kept = jnp.where(norm >= whole[j], 1.0, 0.0)
        sound = kept if j == 0 else jnp.minimum(sound, kept)
        inverse = lax.rsqrt(norm + 1e-06)
        scale = inverse if j == 0 else jnp.where(here[j], inverse, scale)
        if j < MODES - 1:
            square = inverse * inverse
            twice = square * (2.0 - square * norm)
            coef, cross = coefs[j], crosses[j]
            for i in range(j + 1, MODES):
                are, aim = row(coef, i) * twice, row(coef, 4 + i) * twice
                coefs[i] = coefs[i] - (are * coef - aim * cross)
                if i < MODES - 1:
                    crosses[i] = crosses[i] - (are * cross + aim * coef)
            square = jnp.where(later[j], square, 0.0)
            steps.append((coef * square, cross * square))
    return steps, scale, sound


def apply(steps, scale, y, turned):
    for j, (coef, cross) in enumerate(steps):
        vre, vim = row(y, j), row(y, 4 + j)
        y, turned = y - (coef * vre + cross * vim), turned - (coef * vim - cross * vre)
    return y * scale, turned * scale


def modes_kernel(gram_ref, start_ref, high23, low23, high01_hbm, low01_hbm, out_ref, high01, low01, mats_ref, sems):
    fetch = [
        pltpu.make_async_copy(high01_hbm, high01, sems.at[0]),
        pltpu.make_async_copy(low01_hbm, low01, sems.at[1]),
    ]
    for copy in fetch:
        copy.start()
    col = lax.broadcasted_iota(jnp.int32, (128, 128), 1)
    row = lax.broadcasted_iota(jnp.int32, (128, 128), 0)
    lane_row = lax.broadcasted_iota(jnp.int32, (8, 128), 0)
    sign = jnp.where(lane_row < 4, 1.0, -1.0)
    mode = lane_row & 3
    later = [mode > j for j in range(MODES)]
    here = [mode == j for j in range(MODES)]
    for f in range(BINS):
        packed = gram_ref[f * 128 : (f + 1) * 128, :]
        flipped = packed.T
        gram_re = jnp.where(col >= row, packed, flipped)
        gram_im = jnp.where(col < row, packed, jnp.where(col > row, -flipped, 0.0))
        mats_ref[f, 0], mats_ref[f, 1] = split(jnp.concatenate([gram_re, gram_im], 0))
    start = start_ref[...]

    def image_of(f, vec):
        hi, lo = split(jnp.concatenate(vec, 1))
        ghi, glo = mats_ref[f, 0], mats_ref[f, 1]
        prod = dot(jnp.concatenate([hi, lo], 0), ghi, NN)
        image = prod[:8] + prod[8:] + dot(hi, glo, NN)
        return image, sign * pltpu.roll(image, 4, 0)

    first = (start, sign * pltpu.roll(start, 4, 0))

    def iterate_by_columns():
        vecs = [first] * BINS
        for _ in range(ITERS):
            images = [image_of(f, vecs[f]) for f in range(BINS)]
            vecs = []
            for y, turned in images:
                (y, turned), scale = by_columns(y, turned, later, here)
                vecs.append((y * scale, turned * scale))
        return vecs

    def iterate_by_products():
        images = [image_of(f, first) for f in range(BINS)]
        sound = jnp.ones((8, 128), F32)
        for sweep in range(ITERS):
            nexts = [image_of(f, images[f]) for f in range(BINS)] if sweep < ITERS - 1 else images
            found = [by_products(*images[f], later, here) for f in range(BINS)]
            for _, _, kept in found:
                sound = jnp.minimum(sound, kept)
            images = [apply(steps, scale, *nexts[f]) for f, (steps, scale, _) in enumerate(found)]
        return images, sound

    def finish(vecs):
        amps = []
        for f in range(BINS):
            y, turned = vecs[f]
            hi, lo = split(jnp.concatenate([y, -turned], 1))
            high_ref, low_ref = (high01, low01) if f < PAIR else (high23, low23)
            prod = dot(jnp.concatenate([hi, lo], 0), high_ref[f % PAIR], NN)
            amps.append(prod[:8] + prod[8:] + dot(hi, low_ref[f % PAIR], NN))
        for half in range(2):
            rows = []
            for i in range(4 * half, 4 * half + 4):
                for f in range(BINS):
                    rows.append(amps[f][:, i * 128 : (i + 1) * 128])
            out_ref[pl.ds(half, 128, stride=2), :] = jnp.concatenate(rows, 0).T

    vecs, sound = iterate_by_products()
    is_sound = jnp.min(sound) > 0.5
    for copy in fetch:
        copy.wait()
    finish(vecs)

    @pl.when(jnp.logical_not(is_sound))
    def _():
        finish(iterate_by_columns())


def start_basis():
    rowpos = np.arange(NB) + 0.5
    colpos = np.arange(MODES) + 1.0
    basis = np.zeros((8, 128), np.float32)
    basis[:MODES, :NB] = np.cos(math.pi * colpos[:, None] * rowpos[None, :] / NB)
    return jnp.asarray(basis)


def amplitudes(gram, early, late):
    return pl.pallas_call(
        modes_kernel,
        out_shape=jax.ShapeDtypeStruct((2 * DEVICES, 128), F32),
        in_specs=[pl.BlockSpec(memory_space=pltpu.VMEM)] * 4 + [pl.BlockSpec(memory_space=pltpu.HBM)] * 2,
        scratch_shapes=[
            pltpu.VMEM((PAIR, 256, MICS), BF),
            pltpu.VMEM((PAIR, 256, MICS), BF),
            pltpu.VMEM((BINS, 2, 256, 128), BF),
            pltpu.SemaphoreType.DMA((2,)),
        ],
        compiler_params=pltpu.CompilerParams(vmem_limit_bytes=24 << 20),
        name="modes",
    )(gram, start_basis(), *late, *[in_hbm(x) for x in early])


def power_kernel(parts_ref, out_ref):
    total = parts_ref[0:8, :]
    for s in range(1, 32):
        total = total + parts_ref[8 * s : 8 * s + 8, :]
    total = total + pltpu.roll(total, 4, 0)
    total = total + pltpu.roll(total, 6, 0)
    square = total * total
    lane = lax.broadcasted_iota(jnp.int32, (8, 128), 1)
    row = lax.broadcasted_iota(jnp.int32, (8, 128), 0)
    mic = lax.broadcasted_iota(jnp.int32, (8, 8), 1)
    out = jnp.zeros((8, 8), F32)
    for half in range(2):
        source = jnp.broadcast_to(square[half : half + 1, :], (8, 128))
        for i in range(4):
            sums = jnp.sum(jnp.where((lane >> 3) == 4 * i + row, source, 0.0), axis=1, keepdims=True)
            out = jnp.where(mic == 4 * half + i, sums, out)
    out_ref[...] = out[:BINS, :]


def power(parts):
    return pl.pallas_call(
        power_kernel,
        out_shape=jax.ShapeDtypeStruct((BINS, MICS // DEVICES), F32),
        compiler_params=pltpu.CompilerParams(vmem_limit_bytes=4 << 20),
        name="power",
    )(parts).T


def exchange(x):
    return lax.all_to_all(x, AXES, 0, 0, tiled=True)


def on_device(pressure, weights, green_table, starts, bin_index):
    gram, high, low = local_gram(pressure, weights, starts, bin_index)
    parts = exchange(gram.reshape(DEVICES, 4, 128))
    early = project(green_table, high, low, 0, pltpu.HBM)
    parts, early = lax.optimization_barrier((parts, early))
    shared = share_sum(parts.reshape(512, 128))
    shared, high, low = lax.optimization_barrier((shared, high, low))
    summed = exchange(shared.reshape(DEVICES, 4, 128)).reshape(512, 128)
    late = project(green_table, high, low, PAIR, jax.ShapeDtypeStruct)
    partial = amplitudes(summed, early, late)
    return power(exchange(partial.reshape(DEVICES, 2, 128)).reshape(2 * DEVICES, 128))


def solution(mesh):
    return jax.shard_map(
        on_device,
        mesh=mesh,
        in_specs=(
            P(None, AXES),
            P(AXES),
            P(None, None, None, AXES),
            P(),
            P(),
        ),
        out_specs=P(AXES, None),
        check_vma=False,
    )
```
